32 devices in a mesh: blk: 8 (over z, x), group: 4 (over y, core).
Axes of the slice: x: 2, y: 2, z: 4, core: 2. Of those that a mesh axis runs over, the one named last changes fastest.
Arguments:
- activations: bfloat16 [131072, 2048], P(('blk', 'group')), may hold values from -8 to 8
- grad_out: bfloat16 [131072, 512], P(('blk', 'group')), may hold values from -8 to 8
- weights: float32 [2048, 512], P(('blk', 'group')), may hold values from -6 to 6
- momentum: float32 [2048, 512], P(('blk', 'group')), may hold values from -6 to 6
Outputs:
- new_weights: float32 [2048, 512], P(('blk', 'group'))
- new_momentum: float32 [2048, 512], P(('blk', 'group'))
The draws below stay inside these ranges and needn't reach their ends.
All inputs are finite; a program needn't handle non-finite values.
Results may differ from the reference program's by a relative error of at most 0.0003.
Values sent between devices are 32-bit elements; how exact they have to be, the bound alone decides.
A program may use at most 128 MiB of HBM per device.

```python
import math
import jax
import jax.numpy as jnp
from jax import lax

D = 2048
COLS = 512
TOK_DEV = 4096
TOKENS = 131072
LEVELS = 2
N_BLK = 8
N_GROUP = 4


def draw_common(key, width, salt):
    noise_key, offset_key = jax.random.split(jax.random.fold_in(key, salt), 2)
    noise = jax.random.normal(noise_key, (TOKENS, width), jnp.float32)
    offset = jax.random.normal(offset_key, (width,), jnp.float32) * (TOK_DEV * 16.0) ** (-0.25)
    drawn = noise + offset
    return jnp.clip(drawn, -8.0, 8.0)


def draw_activations(key, part):
    return draw_common(key, D, 11).astype(jnp.bfloat16)


def draw_grad_out(key, part):
    return draw_common(key, COLS, 23).astype(jnp.bfloat16)


def steps_of(stream_key, shape, cuts, low, top_value):
    gain, own = 1.0, jax.random.fold_in(stream_key, 6)
    for axis_at, blocks in cuts:
        draws = jnp.exp(jax.random.uniform(jax.random.fold_in(own, axis_at), (blocks,), jnp.float32, low / len(cuts), top_value / len(cuts)))
        gain = gain * jnp.repeat(draws, shape[axis_at] // blocks).reshape([-1 if axis == axis_at else 1 for axis in range(len(shape))])
    return gain


def centred(own_key, shape, scale, limit, pieces=(), kind=jnp.bfloat16):
    loudness = steps_of(own_key, shape, pieces, -0.22, 0.18) if pieces else 1.0
    values = jax.random.normal(own_key, shape, jnp.float32) * scale * loudness
    return jnp.minimum(jnp.maximum(values, -limit), limit).astype(kind)


def setup_inputs(seed: int = 0) -> dict:
    splits = jax.random.split(jax.random.key(seed), 5)
    activations = draw_activations(jax.random.fold_in(splits[4], 71), 0)
    grad_out = draw_grad_out(jax.random.fold_in(splits[4], 71), 0)
    weights = centred(splits[2], (D, COLS), 1.0, 6.0, ((0, 32),), jnp.float32)
    momentum = centred(splits[3], (D, COLS), 1.0, 6.0, ((0, 32),), jnp.float32)
    return dict(activations=activations, grad_out=grad_out, weights=weights, momentum=momentum)


epsilon = 1e-06

def reference(activations, grad_out, weights, momentum):
    act_blocks = activations.reshape(N_BLK, N_GROUP, TOK_DEV, D)
    out_blocks = grad_out.reshape(N_BLK, N_GROUP, TOK_DEV, COLS)
    grad_scale = 1.0 / math.sqrt(TOK_DEV * N_BLK)

    def group_grad(group_index):
        act_group = lax.dynamic_index_in_dim(act_blocks, group_index, 1, keepdims=False).reshape(N_BLK * TOK_DEV, D)
        out_group = lax.dynamic_index_in_dim(out_blocks, group_index, 1, keepdims=False).reshape(N_BLK * TOK_DEV, COLS)
        return jnp.dot(act_group.T, out_group, preferred_element_type=jnp.float32) * grad_scale
    stacked = lax.map(group_grad, jnp.arange(N_GROUP, dtype=jnp.int32))
    for level_step in range(LEVELS):
        half_rows = stacked.shape[0] // 2
        lower_half = stacked[:half_rows]
        upper_half = stacked[half_rows:]
        inner_prod = lax.optimization_barrier(jnp.sum(lower_half * upper_half, axis=(1, 2)))
        lower_sq = lax.optimization_barrier(jnp.sum(lower_half * lower_half, axis=(1, 2)))
        upper_sq = lax.optimization_barrier(jnp.sum(upper_half * upper_half, axis=(1, 2)))
        coef_lower = 1.0 - inner_prod / (2.0 * (lower_sq + epsilon))
        coef_upper = 1.0 - inner_prod / (2.0 * (upper_sq + epsilon))
        stacked = coef_lower[:, None, None] * lower_half + coef_upper[:, None, None] * upper_half
    combined = stacked[0]
    new_momentum = 0.9 * momentum + combined
    new_weights = (1.0 - 0.1 * 0.1) * weights - 0.1 * new_momentum
    return (new_weights, new_momentum)
```

```python
import functools
import math

import jax
import jax.numpy as jnp
from jax import lax
from jax.experimental import pallas as pl
from jax.experimental.pallas import tpu as pltpu
from jax.sharding import PartitionSpec as P

epsilon = 1e-06
MESH = pl.DeviceIdType.MESH
PIECES = 4
FIRST_EVENT_STEP = 3


def flipped(index, mask, bits):
    for bit in range(bits):
        if mask >> bit & 1:
            weight = 1 << bit
            index = index + weight * (1 - 2 * lax.rem(lax.div(index, weight), 2))
    return index


class Plan:
    def __init__(self, blk_count, group_count):
        self.blk_count, self.group_count = blk_count, group_count
        self.blk_bits = blk_count.bit_length() - 1
        self.group_bits = group_count.bit_length() - 1
        self.hs = list(range(group_count - 1, -1, -1))
        self.slots = {}
        for h in self.hs:
            for r in range(blk_count):
                for stage in self.receives(r, h):
                    self.slots[stage, r, h] = len(self.slots)

    def order(self, h):
        return list(range(self.blk_bits))

    def receives(self, r, h):
        sent = self.sends(r, h)
        return range(self.blk_bits if sent is None else sent[0])

    def sends(self, r, h):
        for stage, bit in enumerate(self.order(h)):
            if r >> bit & 1:
                return stage, bit
        return None

    def pairs(self):
        return [(k, l) for k in range(self.group_count) for l in range(k, self.group_count)]


def kernel(
    plan, grad_scale, act_ref, gout_ref, out_ref,
    act_buf, gout_buf, acc, arrived, pieces, gram_own, gram_sum, gram_group, gram_blk,
    act_sem, gout_sem, send_sem, recv_sem, gsend_sem, grecv_sem,
    asend_sem, arecv_sem, bsend_sem, brecv_sem,
):
    b = lax.axis_index("blk")
    g = lax.axis_index("group")
    B, G = plan.blk_count, plan.group_count
    tokens = act_ref.shape[0]
    blk_rows = acc.shape[1] * acc.shape[2]
    cols = acc.shape[3]
    depth = tokens // PIECES
    b_of = [flipped(b, r, plan.blk_bits) for r in range(B)]
    g_of = [flipped(g, h, plan.group_bits) for h in range(G)]

    def act_copy(r, piece):
        rows = pl.ds(pl.multiple_of(piece * depth, depth), depth)
        lanes = pl.ds(pl.multiple_of(b_of[r] * blk_rows, blk_rows), blk_rows)
        return pltpu.make_async_copy(
            act_ref.at[rows, lanes], act_buf.at[r, rows], act_sem.at[r, piece]
        )

    def gout_copy(piece):
        rows = pl.ds(pl.multiple_of(piece * depth, depth), depth)
        return pltpu.make_async_copy(gout_ref.at[rows], gout_buf.at[rows], gout_sem.at[piece])

    for piece in range(PIECES):
        gout_copy(piece).start()
        act_copy(B - 1, piece).start()
    for r in range(B - 2, -1, -1):
        for piece in range(PIECES):
            act_copy(r, piece).start()

    barrier = pltpu.get_barrier_semaphore()
    for r in range(1, B):
        pl.semaphore_signal(barrier, inc=1, device_id=(b_of[r], g), device_id_type=MESH)
    for h in range(1, G):
        pl.semaphore_signal(barrier, inc=1, device_id=(b, g_of[h]), device_id_type=MESH)

    def matmul(r):
        def step(piece, first):
            act_copy(r, piece).wait()
            if r == B - 1:
                gout_copy(piece).wait()
            rows = pl.ds(pl.multiple_of(piece * depth, depth), depth)
            product = lax.dot_general(
                act_buf[r, rows], gout_buf[rows], (((0,), (0,)), ((), ())),
                preferred_element_type=jnp.float32,
            ).reshape(acc.shape[1:])
            if first:
                acc[r] = product
            else:
                acc[r] += product

        step(0, True)

        def body(piece, carry):
            step(piece, False)
            return carry

        lax.fori_loop(1, PIECES, body, 0)

    def block_copy(slot_key):
        stage, r, h = slot_key
        slot = plan.slots[slot_key]
        mask = 1 << plan.order(h)[stage]
        return pltpu.make_async_remote_copy(
            src_ref=acc.at[r ^ mask, g_of[h]],
            dst_ref=arrived.at[slot],
            send_sem=send_sem.at[slot],
            recv_sem=recv_sem.at[slot],
            device_id=(b_of[mask], g),
            device_id_type=MESH,
        )

    def group_copy(h):
        return pltpu.make_async_remote_copy(
            src_ref=acc.at[0, g_of[h]],
            dst_ref=pieces.at[h],
            send_sem=gsend_sem.at[h],
            recv_sem=grecv_sem.at[h],
            device_id=(b, g_of[h]),
            device_id_type=MESH,
        )

    def send(r, h):
        stage, bit = plan.sends(r, h)
        block_copy((stage, r ^ (1 << bit), h)).start()

    def process(r, h):
        keys = [(stage, r, h) for stage in plan.receives(r, h)]
        total = acc[r, g_of[h]]
        for key in keys:
            block_copy(key).wait_recv()
            total = total + arrived[plan.slots[key]]
        if r:
            acc[r, g_of[h]] = total
            send(r, h)
        elif h:
            acc[0, g_of[h]] = total * grad_scale
            group_copy(h).start()
        else:
            pieces[0] = total * grad_scale

    pending = []
    for step in range(B):
        r = B - 1 - step
        matmul(r)
        if step == 0:
            pl.semaphore_wait(barrier, B - 1 + G - 1)
        for h in plan.hs:
            if len(plan.receives(r, h)) == 0:
                send(r, h)
            else:
                pending.append((r, h))
        if step >= FIRST_EVENT_STEP and step < B - 1:
            process(*pending.pop(0))
    for r, h in pending:
        process(r, h)

    for h in range(1, G):
        group_copy(h).wait_recv()
    pairs = plan.pairs()
    place = [flipped(g, k, plan.group_bits) for k in range(G)]
    for at, (k, l) in enumerate(pairs):
        gram_own[pl.ds(at, 1), :] = jnp.sum(
            jnp.sum(pieces[place[k]] * pieces[place[l]], axis=0, keepdims=True).reshape(1, cols // 128, 128),
            axis=1,
        )
    for at in range(len(pairs), gram_own.shape[0]):
        gram_own[pl.ds(at, 1), :] = jnp.zeros((1, 128), jnp.float32)

    def gram_copy_group(h):
        return pltpu.make_async_remote_copy(
            src_ref=gram_own, dst_ref=gram_group.at[h],
            send_sem=asend_sem.at[h], recv_sem=arecv_sem.at[h],
            device_id=(b, g_of[h]), device_id_type=MESH,
        )

    def gram_copy_blk(r):
        return pltpu.make_async_remote_copy(
            src_ref=gram_sum, dst_ref=gram_blk.at[r],
            send_sem=bsend_sem.at[r], recv_sem=brecv_sem.at[r],
            device_id=(b_of[r], g), device_id_type=MESH,
        )

    for h in range(G - 1, 0, -1):
        gram_copy_group(h).start()
    total = gram_own[...]
    for h in range(1, G):
        gram_copy_group(h).wait_recv()
        total = total + gram_group[h]
    gram_sum[...] = total
    for r in range(B - 1, 0, -1):
        gram_copy_blk(r).start()
    for r in range(1, B):
        gram_copy_blk(r).wait_recv()
        total = total + gram_blk[r]
    sums = jnp.sum(total, axis=1, keepdims=True)
    gram = {}
    for at, (k, l) in enumerate(pairs):
        gram[k, l] = gram[l, k] = sums[at:at + 1]

    def product(first, second):
        result = None
        for k, weight in first.items():
            inner = None
            for l, other in second.items():
                term = gram[k, l] if other is None else other * gram[k, l]
                inner = term if inner is None else inner + term
            inner = inner if weight is None else weight * inner
            result = inner if result is None else result + inner
        return result

    entries = [{k: None} for k in range(G)]
    while len(entries) > 1:
        half = len(entries) // 2
        merged = []
        for i in range(half):
            first, second = entries[i], entries[i + half]
            inner = product(first, second)
            first_sq = jnp.maximum(product(first, first), 0.0)
            second_sq = jnp.maximum(product(second, second), 0.0)
            coef_first = 1.0 - inner / (2.0 * (first_sq + epsilon))
            coef_second = 1.0 - inner / (2.0 * (second_sq + epsilon))
            entry = {}
            for source, coef in ((first, coef_first), (second, coef_second)):
                for k, weight in source.items():
                    entry[k] = coef if weight is None else coef * weight
            merged.append(entry)
        entries = merged
    combined = None
    for k, weight in entries[0].items():
        term = weight * pieces[place[k]]
        combined = term if combined is None else combined + term
    out_ref[...] = combined

    for key in plan.slots:
        block_copy(key).wait_send()
    for h in range(1, G):
        group_copy(h).wait_send()
        gram_copy_group(h).wait_send()
    for r in range(1, B):
        gram_copy_blk(r).wait_send()


def shards(blk_count, group_count, activations, grad_out, weights, momentum):
    plan = Plan(blk_count, group_count)
    tok_rows, width = activations.shape
    cols = grad_out.shape[1]
    sub_rows = width // (blk_count * group_count)
    blk_rows = sub_rows * group_count
    grad_scale = 1.0 / math.sqrt(tok_rows * blk_count)
    gram_rows = -(-len(plan.pairs()) // 8) * 8
    dma = pltpu.SemaphoreType.DMA
    f32 = jnp.float32
    combined = pl.pallas_call(
        functools.partial(kernel, plan, grad_scale),
        out_shape=jax.ShapeDtypeStruct((sub_rows, cols), f32),
        in_specs=[pl.BlockSpec(memory_space=pl.ANY)] * 2,
        out_specs=pl.BlockSpec(memory_space=pltpu.VMEM),
        scratch_shapes=[
            pltpu.VMEM((blk_count, tok_rows, blk_rows), activations.dtype),
            pltpu.VMEM((tok_rows, cols), grad_out.dtype),
            pltpu.VMEM((blk_count, group_count, sub_rows, cols), f32),
            pltpu.VMEM((len(plan.slots), sub_rows, cols), f32),
            pltpu.VMEM((group_count, sub_rows, cols), f32),
            pltpu.VMEM((gram_rows, 128), f32),
            pltpu.VMEM((gram_rows, 128), f32),
            pltpu.VMEM((group_count, gram_rows, 128), f32),
            pltpu.VMEM((blk_count, gram_rows, 128), f32),
            dma((blk_count, PIECES)),
            dma((PIECES,)),
            dma((len(plan.slots),)),
            dma((len(plan.slots),)),
            dma((group_count,)),
            dma((group_count,)),
            dma((group_count,)),
            dma((group_count,)),
            dma((blk_count,)),
            dma((blk_count,)),
        ],
        compiler_params=pltpu.CompilerParams(
            collective_id=0, has_side_effects=True, vmem_limit_bytes=50 * 1024 * 1024
        ),
        name="adasum",
    )(activations, grad_out)
    new_momentum = 0.9 * momentum + combined
    new_weights = (1.0 - 0.1 * 0.1) * weights - 0.1 * new_momentum
    return (new_weights, new_momentum)


def solution(mesh):
    spec = P(("blk", "group"), None)
    body = functools.partial(shards, mesh.shape["blk"], mesh.shape["group"])
    return jax.shard_map(
        body, mesh=mesh, in_specs=(spec,) * 4, out_specs=(spec,) * 2, check_vma=False
    )
```

```python
import functools
import math

import jax
import jax.numpy as jnp
from jax import lax
from jax.experimental import pallas as pl
from jax.experimental.pallas import tpu as pltpu
from jax.sharding import PartitionSpec as P

epsilon = 1e-06
MESH = pl.DeviceIdType.MESH
PIECES = 4
FIRST_EVENT_STEP = 3


def flipped(index, mask, bits):
    for bit in range(bits):
        if mask >> bit & 1:
            weight = 1 << bit
            index = index + weight * (1 - 2 * lax.rem(lax.div(index, weight), 2))
    return index


class Plan:
    def __init__(self, blk_count, group_count):
        self.blk_count, self.group_count = blk_count, group_count
        self.blk_bits = blk_count.bit_length() - 1
        self.group_bits = group_count.bit_length() - 1
        self.hs = list(range(group_count - 1, -1, -1))
        self.mixed = blk_count == 8
        self.slots = {}
        for h in self.hs:
            for r in range(blk_count):
                for stage in self.receives(r, h):
                    self.slots[stage, r, h] = len(self.slots)

    def order(self, h):
        bits = list(range(self.blk_bits))
        if self.mixed and h == self.hs[0]:
            bits[:2] = bits[1::-1]
        return bits

    def receives(self, r, h):
        sent = self.sends(r, h)
        return range(self.blk_bits if sent is None else sent[0])

    def sends(self, r, h):
        for stage, bit in enumerate(self.order(h)):
            if r >> bit & 1:
                return stage, bit
        return None

    def schedule(self):
        if self.mixed:
            return self.mixed_schedule()
        steps, pending = [], []
        for r in range(self.blk_count - 1, -1, -1):
            steps.append(("matmul", r, None))
            for h in self.hs:
                if len(self.receives(r, h)) == 0:
                    steps.append(("send", r, h))
                else:
                    pending.append(("process", r, h))
            if r < self.blk_count - FIRST_EVENT_STEP and r > 0:
                steps.append(pending.pop(0))
        return steps + pending

    def mixed_schedule(self):
        steps = []
        first, rest = self.hs[0], self.hs[1:]

        def matmul(r):
            steps.append(("matmul", r, None))

        def add(kind, r, hs):
            steps.extend((kind, r, h) for h in hs)

        matmul(7)
        add("send", 7, [first] + rest)
        matmul(6)
        add("send", 6, [first])
        matmul(3)
        add("send", 3, [first])
        matmul(5)
        add("send", 5, rest)
        add("process", 5, [first])
        add("send", 3, rest)
        add("process", 6, rest[:1])
        matmul(2)
        add("send", 2, [first])
        matmul(1)
        add("process", 6, rest[1:2])
        add("process", 1, [first])
        add("send", 1, rest)
        matmul(4)
        add("process", 6, rest[2:])
        matmul(0)
        add("process", 4, [first] + rest)
        add("process", 2, rest)
        add("process", 0, [first] + rest)
        return steps

    def pairs(self):
        return [(k, l) for k in range(self.group_count) for l in range(k, self.group_count)]


def kernel(
    plan, grad_scale, act_ref, gout_ref, out_ref,
    act_buf, gout_buf, acc, arrived, pieces, gram_own, gram_sum, gram_group, gram_blk,
    act_sem, gout_sem, send_sem, recv_sem, gsend_sem, grecv_sem,
    asend_sem, arecv_sem, bsend_sem, brecv_sem,
):
    b = lax.axis_index("blk")
    g = lax.axis_index("group")
    B, G = plan.blk_count, plan.group_count
    tokens = act_ref.shape[0]
    blk_rows = acc.shape[1] * acc.shape[2]
    cols = acc.shape[3]
    depth = tokens // PIECES
    b_of = [flipped(b, r, plan.blk_bits) for r in range(B)]
    g_of = [flipped(g, h, plan.group_bits) for h in range(G)]

    def act_copy(r, piece):
        rows = pl.ds(pl.multiple_of(piece * depth, depth), depth)
        lanes = pl.ds(pl.multiple_of(b_of[r] * blk_rows, blk_rows), blk_rows)
        return pltpu.make_async_copy(
            act_ref.at[rows, lanes], act_buf.at[r, rows], act_sem.at[r, piece]
        )

    def gout_copy(piece):
        rows = pl.ds(pl.multiple_of(piece * depth, depth), depth)
        return pltpu.make_async_copy(gout_ref.at[rows], gout_buf.at[rows], gout_sem.at[piece])

    steps = plan.schedule()
    loads = [r for kind, r, h in steps if kind == "matmul"]

    def prefetch(at):
        if at < B:
            for piece in range(PIECES):
                act_copy(loads[at], piece).start()

    for piece in range(PIECES):
        gout_copy(piece).start()
        act_copy(loads[0], piece).start()

    barrier = pltpu.get_barrier_semaphore()
    for r in range(1, B):
        pl.semaphore_signal(barrier, inc=1, device_id=(b_of[r], g), device_id_type=MESH)
    for h in range(1, G):
        pl.semaphore_signal(barrier, inc=1, device_id=(b, g_of[h]), device_id_type=MESH)

    def matmul(r):
        def step(piece, first):
            act_copy(r, piece).wait()
            if r == loads[0]:
                gout_copy(piece).wait()
            rows = pl.ds(pl.multiple_of(piece * depth, depth), depth)
            product = lax.dot_general(
                act_buf[r, rows], gout_buf[rows], (((0,), (0,)), ((), ())),
                preferred_element_type=jnp.float32,
            ).reshape(acc.shape[1:])
            if first:
                acc[r] = product
            else:
                acc[r] += product

        step(0, True)
        if r == loads[0]:
            prefetch(1)

        def body(piece, carry):
            step(piece, False)
            return carry

        lax.fori_loop(1, PIECES, body, 0)

    def block_copy(slot_key):
        stage, r, h = slot_key
        slot = plan.slots[slot_key]
        mask = 1 << plan.order(h)[stage]
        return pltpu.make_async_remote_copy(
            src_ref=acc.at[r ^ mask, g_of[h]],
            dst_ref=arrived.at[slot],
            send_sem=send_sem.at[slot],
            recv_sem=recv_sem.at[slot],
            device_id=(b_of[mask], g),
            device_id_type=MESH,
        )

    def group_copy(h):
        return pltpu.make_async_remote_copy(
            src_ref=acc.at[0, g_of[h]],
            dst_ref=pieces.at[h],
            send_sem=gsend_sem.at[h],
            recv_sem=grecv_sem.at[h],
            device_id=(b, g_of[h]),
            device_id_type=MESH,
        )

    def send(r, h):
        stage, bit = plan.sends(r, h)
        block_copy((stage, r ^ (1 << bit), h)).start()

    def process(r, h):
        keys = [(stage, r, h) for stage in plan.receives(r, h)]
        total = acc[r, g_of[h]]
        for key in keys:
            block_copy(key).wait_recv()
            total = total + arrived[plan.slots[key]]
        if r:
            acc[r, g_of[h]] = total
            send(r, h)
        elif h:
            acc[0, g_of[h]] = total * grad_scale
            group_copy(h).start()
        else:
            pieces[0] = total * grad_scale

    done = 0
    for kind, r, h in steps:
        if kind == "matmul":
            if done:
                prefetch(done + 1)
            matmul(r)
            done += 1
            if done == 1:
                pl.semaphore_wait(barrier, B - 1 + G - 1)
        elif kind == "send":
            send(r, h)
        else:
            process(r, h)

    for h in range(1, G):
        group_copy(h).wait_recv()
    pairs = plan.pairs()
    place = [flipped(g, k, plan.group_bits) for k in range(G)]
    for at, (k, l) in enumerate(pairs):
        gram_own[pl.ds(at, 1), :] = jnp.sum(
            jnp.sum(pieces[place[k]] * pieces[place[l]], axis=0, keepdims=True).reshape(1, cols // 128, 128),
            axis=1,
        )
    for at in range(len(pairs), gram_own.shape[0]):
        gram_own[pl.ds(at, 1), :] = jnp.zeros((1, 128), jnp.float32)

    def gram_copy_group(h):
        return pltpu.make_async_remote_copy(
            src_ref=gram_own, dst_ref=gram_group.at[h],
            send_sem=asend_sem.at[h], recv_sem=arecv_sem.at[h],
            device_id=(b, g_of[h]), device_id_type=MESH,
        )

    def gram_copy_blk(r):
        return pltpu.make_async_remote_copy(
            src_ref=gram_sum, dst_ref=gram_blk.at[r],
            send_sem=bsend_sem.at[r], recv_sem=brecv_sem.at[r],
            device_id=(b_of[r], g), device_id_type=MESH,
        )

    for h in range(G - 1, 0, -1):
        gram_copy_group(h).start()
    total = gram_own[...]
    for h in range(1, G):
        gram_copy_group(h).wait_recv()
        total = total + gram_group[h]
    gram_sum[...] = total
    for r in range(B - 1, 0, -1):
        gram_copy_blk(r).start()
    for r in range(1, B):
        gram_copy_blk(r).wait_recv()
        total = total + gram_blk[r]
    sums = jnp.sum(total, axis=1, keepdims=True)
    gram = {}
    for at, (k, l) in enumerate(pairs):
        gram[k, l] = gram[l, k] = sums[at:at + 1]

    def product(first, second):
        result = None
        for k, weight in first.items():
            inner = None
            for l, other in second.items():
                term = gram[k, l] if other is None else other * gram[k, l]
                inner = term if inner is None else inner + term
            inner = inner if weight is None else weight * inner
            result = inner if result is None else result + inner
        return result

    entries = [{k: None} for k in range(G)]
    while len(entries) > 1:
        half = len(entries) // 2
        merged = []
        for i in range(half):
            first, second = entries[i], entries[i + half]
            inner = product(first, second)
            first_sq = jnp.maximum(product(first, first), 0.0)
            second_sq = jnp.maximum(product(second, second), 0.0)
            coef_first = 1.0 - inner / (2.0 * (first_sq + epsilon))
            coef_second = 1.0 - inner / (2.0 * (second_sq + epsilon))
            entry = {}
            for source, coef in ((first, coef_first), (second, coef_second)):
                for k, weight in source.items():
                    entry[k] = coef if weight is None else coef * weight
            merged.append(entry)
        entries = merged
    combined = None
    for k, weight in entries[0].items():
        term = weight * pieces[place[k]]
        combined = term if combined is None else combined + term
    out_ref[...] = combined

    for key in plan.slots:
        block_copy(key).wait_send()
    for h in range(1, G):
        group_copy(h).wait_send()
        gram_copy_group(h).wait_send()
    for r in range(1, B):
        gram_copy_blk(r).wait_send()


def shards(blk_count, group_count, activations, grad_out, weights, momentum):
    plan = Plan(blk_count, group_count)
    tok_rows, width = activations.shape
    cols = grad_out.shape[1]
    sub_rows = width // (blk_count * group_count)
    blk_rows = sub_rows * group_count
    grad_scale = 1.0 / math.sqrt(tok_rows * blk_count)
    gram_rows = -(-len(plan.pairs()) // 8) * 8
    dma = pltpu.SemaphoreType.DMA
    f32 = jnp.float32
    combined = pl.pallas_call(
        functools.partial(kernel, plan, grad_scale),
        out_shape=jax.ShapeDtypeStruct((sub_rows, cols), f32),
        in_specs=[pl.BlockSpec(memory_space=pl.ANY)] * 2,
        out_specs=pl.BlockSpec(memory_space=pltpu.VMEM),
        scratch_shapes=[
            pltpu.VMEM((blk_count, tok_rows, blk_rows), activations.dtype),
            pltpu.VMEM((tok_rows, cols), grad_out.dtype),
            pltpu.VMEM((blk_count, group_count, sub_rows, cols), f32),
            pltpu.VMEM((len(plan.slots), sub_rows, cols), f32),
            pltpu.VMEM((group_count, sub_rows, cols), f32),
            pltpu.VMEM((gram_rows, 128), f32),
            pltpu.VMEM((gram_rows, 128), f32),
            pltpu.VMEM((group_count, gram_rows, 128), f32),
            pltpu.VMEM((blk_count, gram_rows, 128), f32),
            dma((blk_count, PIECES)),
            dma((PIECES,)),
            dma((len(plan.slots),)),
            dma((len(plan.slots),)),
            dma((group_count,)),
            dma((group_count,)),
            dma((group_count,)),
            dma((group_count,)),
            dma((blk_count,)),
            dma((blk_count,)),
        ],
        compiler_params=pltpu.CompilerParams(
            collective_id=0, has_side_effects=True, vmem_limit_bytes=50 * 1024 * 1024
        ),
        name="adasum",
    )(activations, grad_out)
    new_momentum = 0.9 * momentum + combined
    new_weights = (1.0 - 0.1 * 0.1) * weights - 0.1 * new_momentum
    return (new_weights, new_momentum)


def solution(mesh):
    spec = P(("blk", "group"), None)
    body = functools.partial(shards, mesh.shape["blk"], mesh.shape["group"])
    return jax.shard_map(
        body, mesh=mesh, in_specs=(spec,) * 4, out_specs=(spec,) * 2, check_vma=False
    )
```

```python
import functools
import math

import jax
import jax.numpy as jnp
from jax import lax
from jax.experimental import pallas as pl
from jax.experimental.pallas import tpu as pltpu
from jax.sharding import PartitionSpec as P

epsilon = 1e-06
MESH = pl.DeviceIdType.MESH
PIECES = 4
FIRST_EVENT_STEP = 3


def flipped(index, mask, bits):
    for bit in range(bits):
        if mask >> bit & 1:
            weight = 1 << bit
            index = index + weight * (1 - 2 * lax.rem(lax.div(index, weight), 2))
    return index


class Plan:
    def __init__(self, blk_count, group_count):
        self.blk_count, self.group_count = blk_count, group_count
        self.blk_bits = blk_count.bit_length() - 1
        self.group_bits = group_count.bit_length() - 1
        self.hs = list(range(group_count - 1, -1, -1))
        self.mixed = blk_count == 8
        self.slots = {}
        for h in self.hs:
            for r in range(blk_count):
                for stage in self.receives(r, h):
                    self.slots[stage, r, h] = len(self.slots)

    def order(self, h):
        bits = list(range(self.blk_bits))
        if self.mixed and h == self.hs[0]:
            bits[:2] = bits[1::-1]
        return bits

    def receives(self, r, h):
        sent = self.sends(r, h)
        return range(self.blk_bits if sent is None else sent[0])

    def sends(self, r, h):
        for stage, bit in enumerate(self.order(h)):
            if r >> bit & 1:
                return stage, bit
        return None

    def schedule(self):
        if self.mixed:
            return self.mixed_schedule()
        steps, pending = [], []
        for r in range(self.blk_count - 1, -1, -1):
            steps.append(("matmul", r, None))
            for h in self.hs:
                if len(self.receives(r, h)) == 0:
                    steps.append(("send", r, h))
                else:
                    pending.append(("process", r, h))
            if r < self.blk_count - FIRST_EVENT_STEP and r > 0:
                steps.append(pending.pop(0))
        return steps + pending

    def mixed_schedule(self):
        steps = []
        first, rest = self.hs[0], self.hs[1:]

        def matmul(r):
            steps.append(("matmul", r, None))

        def add(kind, r, hs):
            steps.extend((kind, r, h) for h in hs)

        matmul(7)
        add("send", 7, [first] + rest)
        matmul(6)
        add("send", 6, [first])
        matmul(3)
        add("send", 3, [first])
        matmul(5)
        add("send", 5, rest)
        add("process", 5, [first])
        add("send", 3, rest)
        add("process", 6, rest[:1])
        matmul(2)
        add("send", 2, [first])
        matmul(1)
        add("process", 6, rest[1:2])
        add("process", 1, [first])
        add("send", 1, rest)
        matmul(4)
        add("process", 6, rest[2:])
        matmul(0)
        add("process", 4, rest[:2] + [first] + rest[2:])
        add("process", 2, rest)
        add("process", 0, [first] + rest)
        return steps

    def pairs(self):
        return [(k, l) for k in range(self.group_count) for l in range(k, self.group_count)]


def kernel(
    plan, grad_scale, act_ref, gout_ref, out_ref,
    act_buf, gout_buf, acc, arrived, pieces, gram_own, gram_sum, gram_group, gram_blk,
    act_sem, gout_sem, send_sem, recv_sem, gsend_sem, grecv_sem,
    asend_sem, arecv_sem, bsend_sem, brecv_sem,
):
    b = lax.axis_index("blk")
    g = lax.axis_index("group")
    B, G = plan.blk_count, plan.group_count
    tokens = act_ref.shape[0]
    blk_rows = acc.shape[1] * acc.shape[2]
    cols = acc.shape[3]
    depth = tokens // PIECES
    b_of = [flipped(b, r, plan.blk_bits) for r in range(B)]
    g_of = [flipped(g, h, plan.group_bits) for h in range(G)]

    def act_copy(r, piece):
        rows = pl.ds(pl.multiple_of(piece * depth, depth), depth)
        lanes = pl.ds(pl.multiple_of(b_of[r] * blk_rows, blk_rows), blk_rows)
        return pltpu.make_async_copy(
            act_ref.at[rows, lanes], act_buf.at[r, rows], act_sem.at[r, piece]
        )

    def gout_copy(piece):
        rows = pl.ds(pl.multiple_of(piece * depth, depth), depth)
        return pltpu.make_async_copy(gout_ref.at[rows], gout_buf.at[rows], gout_sem.at[piece])

    steps = plan.schedule()
    loads = [r for kind, r, h in steps if kind == "matmul"]

    def prefetch(at):
        if at < B:
            for piece in range(PIECES):
                act_copy(loads[at], piece).start()

    for piece in range(PIECES):
        gout_copy(piece).start()
        act_copy(loads[0], piece).start()

    barrier = pltpu.get_barrier_semaphore()
    for r in range(1, B):
        pl.semaphore_signal(barrier, inc=1, device_id=(b_of[r], g), device_id_type=MESH)
    for h in range(1, G):
        pl.semaphore_signal(barrier, inc=1, device_id=(b, g_of[h]), device_id_type=MESH)

    def matmul(r):
        def step(piece, first):
            act_copy(r, piece).wait()
            if r == loads[0]:
                gout_copy(piece).wait()
            rows = pl.ds(pl.multiple_of(piece * depth, depth), depth)
            product = lax.dot_general(
                act_buf[r, rows], gout_buf[rows], (((0,), (0,)), ((), ())),
                preferred_element_type=jnp.float32,
            ).reshape(acc.shape[1:])
            if first:
                acc[r] = product
            else:
                acc[r] += product

        step(0, True)
        if r == loads[0]:
            prefetch(1)

        def body(piece, carry):
            step(piece, False)
            return carry

        lax.fori_loop(1, PIECES, body, 0)

    def block_copy(slot_key):
        stage, r, h = slot_key
        slot = plan.slots[slot_key]
        mask = 1 << plan.order(h)[stage]
        return pltpu.make_async_remote_copy(
            src_ref=acc.at[r ^ mask, g_of[h]],
            dst_ref=arrived.at[slot],
            send_sem=send_sem.at[slot],
            recv_sem=recv_sem.at[slot],
            device_id=(b_of[mask], g),
            device_id_type=MESH,
        )

    def group_copy(h):
        return pltpu.make_async_remote_copy(
            src_ref=acc.at[0, g_of[h]],
            dst_ref=pieces.at[h],
            send_sem=gsend_sem.at[h],
            recv_sem=grecv_sem.at[h],
            device_id=(b, g_of[h]),
            device_id_type=MESH,
        )

    def send(r, h):
        stage, bit = plan.sends(r, h)
        block_copy((stage, r ^ (1 << bit), h)).start()

    def process(r, h):
        keys = [(stage, r, h) for stage in plan.receives(r, h)]
        total = acc[r, g_of[h]]
        for key in keys:
            block_copy(key).wait_recv()
            total = total + arrived[plan.slots[key]]
        if r:
            acc[r, g_of[h]] = total
            send(r, h)
        elif h:
            acc[0, g_of[h]] = total * grad_scale
            group_copy(h).start()
        else:
            pieces[0] = total * grad_scale

    done = 0
    for kind, r, h in steps:
        if kind == "matmul":
            if done:
                prefetch(done + 1)
            matmul(r)
            done += 1
            if done == 1:
                pl.semaphore_wait(barrier, B - 1 + G - 1)
        elif kind == "send":
            send(r, h)
        else:
            process(r, h)

    for h in range(1, G):
        group_copy(h).wait_recv()
    pairs = plan.pairs()
    place = [flipped(g, k, plan.group_bits) for k in range(G)]
    lane = lax.broadcasted_iota(jnp.int32, gram_own.shape, 1)
    total = jnp.zeros(gram_own.shape, jnp.float32)
    for at, (k, l) in enumerate(pairs):
        inner = jnp.sum(pieces[place[k]] * pieces[place[l]], axis=0, keepdims=True)
        total = total + jnp.where(lane == at, jnp.sum(inner, axis=1, keepdims=True), 0.0)
    gram_own[...] = total

    def gram_copy_group(h):
        return pltpu.make_async_remote_copy(
            src_ref=gram_own, dst_ref=gram_group.at[h],
            send_sem=asend_sem.at[h], recv_sem=arecv_sem.at[h],
            device_id=(b, g_of[h]), device_id_type=MESH,
        )

    def gram_copy_blk(r):
        return pltpu.make_async_remote_copy(
            src_ref=gram_sum, dst_ref=gram_blk.at[r],
            send_sem=bsend_sem.at[r], recv_sem=brecv_sem.at[r],
            device_id=(b_of[r], g), device_id_type=MESH,
        )

    for h in range(G - 1, 0, -1):
        gram_copy_group(h).start()
    for h in range(1, G):
        gram_copy_group(h).wait_recv()
        total = total + gram_group[h]
    gram_sum[...] = total
    for r in range(B - 1, 0, -1):
        gram_copy_blk(r).start()
    for r in range(1, B):
        gram_copy_blk(r).wait_recv()
        total = total + gram_blk[r]
    gram = {}
    for at, (k, l) in enumerate(pairs):
        gram[k, l] = gram[l, k] = jnp.sum(
            jnp.where(lane == at, total, 0.0), axis=1, keepdims=True
        )

    def product(first, second):
        result = None
        for k, weight in first.items():
            inner = None
            for l, other in second.items():
                term = gram[k, l] if other is None else other * gram[k, l]
                inner = term if inner is None else inner + term
            inner = inner if weight is None else weight * inner
            result = inner if result is None else result + inner
        return result

    entries = [{k: None} for k in range(G)]
    while len(entries) > 1:
        half = len(entries) // 2
        merged = []
        for i in range(half):
            first, second = entries[i], entries[i + half]
            inner = product(first, second)
            first_sq = jnp.maximum(product(first, first), 0.0)
            second_sq = jnp.maximum(product(second, second), 0.0)
            coef_first = 1.0 - inner / (2.0 * (first_sq + epsilon))
            coef_second = 1.0 - inner / (2.0 * (second_sq + epsilon))
            entry = {}
            for source, coef in ((first, coef_first), (second, coef_second)):
                for k, weight in source.items():
                    entry[k] = coef if weight is None else coef * weight
            merged.append(entry)
        entries = merged
    combined = None
    for k, weight in entries[0].items():
        term = weight * pieces[place[k]]
        combined = term if combined is None else combined + term
    out_ref[...] = combined

    for key in plan.slots:
        block_copy(key).wait_send()
    for h in range(1, G):
        group_copy(h).wait_send()
        gram_copy_group(h).wait_send()
    for r in range(1, B):
        gram_copy_blk(r).wait_send()


def shards(blk_count, group_count, activations, grad_out, weights, momentum):
    plan = Plan(blk_count, group_count)
    tok_rows, width = activations.shape
    cols = grad_out.shape[1]
    sub_rows = width // (blk_count * group_count)
    blk_rows = sub_rows * group_count
    grad_scale = 1.0 / math.sqrt(tok_rows * blk_count)
    gram_lanes = -(-len(plan.pairs()) // 128) * 128
    dma = pltpu.SemaphoreType.DMA
    f32 = jnp.float32
    combined = pl.pallas_call(
        functools.partial(kernel, plan, grad_scale),
        out_shape=jax.ShapeDtypeStruct((sub_rows, cols), f32),
        in_specs=[pl.BlockSpec(memory_space=pl.ANY)] * 2,
        out_specs=pl.BlockSpec(memory_space=pltpu.VMEM),
        scratch_shapes=[
            pltpu.VMEM((blk_count, tok_rows, blk_rows), activations.dtype),
            pltpu.VMEM((tok_rows, cols), grad_out.dtype),
            pltpu.VMEM((blk_count, group_count, sub_rows, cols), f32),
            pltpu.VMEM((len(plan.slots), sub_rows, cols), f32),
            pltpu.VMEM((group_count, sub_rows, cols), f32),
            pltpu.VMEM((1, gram_lanes), f32),
            pltpu.VMEM((1, gram_lanes), f32),
            pltpu.VMEM((group_count, 1, gram_lanes), f32),
            pltpu.VMEM((blk_count, 1, gram_lanes), f32),
            dma((blk_count, PIECES)),
            dma((PIECES,)),
            dma((len(plan.slots),)),
            dma((len(plan.slots),)),
            dma((group_count,)),
            dma((group_count,)),
            dma((group_count,)),
            dma((group_count,)),
            dma((blk_count,)),
            dma((blk_count,)),
        ],
        compiler_params=pltpu.CompilerParams(
            collective_id=0, has_side_effects=True, vmem_limit_bytes=50 * 1024 * 1024
        ),
        name="adasum",
    )(activations, grad_out)
    new_momentum = 0.9 * momentum + combined
    new_weights = (1.0 - 0.1 * 0.1) * weights - 0.1 * new_momentum
    return (new_weights, new_momentum)


def solution(mesh):
    spec = P(("blk", "group"), None)
    body = functools.partial(shards, mesh.shape["blk"], mesh.shape["group"])
    return jax.shard_map(
        body, mesh=mesh, in_specs=(spec,) * 4, out_specs=(spec,) * 2, check_vma=False
    )
```
